32 devices in a mesh: group: 2 (over x), frame: 4 (over y, core), row: 4 (over z).
Axes of the slice: x: 2, y: 2, z: 4, core: 2. Of those that a mesh axis runs over, the one named last changes fastest.
Arguments:
- latents: bfloat16 [48, 8, 64, 320], P(('group', 'frame'), 'row'), parts along dimension 0, may hold values from -8 to 8
- condition: bfloat16 [24, 8, 64, 320], P(('group', 'frame'), 'row'), parts along dimension 0, may hold values from -6 to 6
- key_frames: int32 [24], P('group'), parts along dimension 0, may hold values from -1 to 23, as said below
- propagate: int32 [48], P('group'), parts along dimension 0, may hold values from 0 to 11, as said below
- encoder_conv: bfloat16 [9, 320, 320], replicated, may hold values from -0.109375 to 0.109375
- zero_conv: bfloat16 [320, 320], replicated, may hold values from -0.3125 to 0.3125
- attention_gain: float32 [320], replicated, may hold values from 0.25 to 1.75
- query_weight: bfloat16 [320, 320], replicated, may hold values from -3 to 3
- key_weight: bfloat16 [320, 320], replicated, may hold values from -3 to 3
- value_weight: bfloat16 [320, 320], replicated, may hold values from -0.3125 to 0.3125
- output_weight: bfloat16 [320, 320], replicated, may hold values from -0.3125 to 0.3125
- conv_gain: float32 [320], replicated, may hold values from 0.25 to 1.75
- block_conv: bfloat16 [9, 320, 320], replicated, may hold values from -0.109375 to 0.109375
Outputs:
- updated: bfloat16 [48, 8, 64, 320], P(('group', 'frame'), 'row'), parts along dimension 0
The draws below stay inside these ranges and needn't reach their ends.
There are 2 independent parts, one for each index of `group`. The reference program is written for one: setup_inputs(seed, part) draws one part's arguments, and reference() takes and returns one part's arrays. A program takes and returns all parts, laid end to end along the dimension named above; an argument that names none is the same for every part. Nothing has to cross between parts.
Inputs may be any that keep to these rules, and one draw needn't show every extreme that they name: `key_frames`: the 3 slots of index d of frame hold keyframes of frames d * 6 to (d + 1) * 6 - 1, all different, live slots first; of index d and the index half the frame axis away, one holds 3 live keyframes and the other 1. `propagate`: each frame names a live slot of its own index of frame or of an adjacent one (no wrap); a keyframe's own frame names its own slot.
All inputs are finite; a program needn't handle non-finite values.
Results may differ from the reference program's by a relative error of at most 0.014.
Values may be sent and summed in bfloat16 or wider, within the bound.
No kernel may reach another device: no remote copies, remote signals or barrier semaphores. Data moves between devices by JAX's collectives and lax.ppermute only.
A program may use at most 64 MiB of HBM per device.

```python
import math
import jax
import jax.numpy as jnp
from jax import lax

C = 320
HEADS = 8
WIDTH = 64
FRAMES_DEV = 6
KEY_LOW = 1
KEY_SLOTS = 3
FRAMES = 24
HEIGHT = 8
KEYS = 12
N_FRAME = 4


def plan_keys(key):
    seeded = jax.random.fold_in(key, 7)
    key_busy, key_perm, key_side, key_pick = jax.random.split(seeded, 4)
    pair_count = N_FRAME // 2
    devices = jnp.arange(N_FRAME, dtype=jnp.int32)
    coin_flip = jax.random.randint(key_busy, (pair_count,), 0, 2)
    lower_half = devices < pair_count
    partner_coin = coin_flip[devices % pair_count]
    crowded = jnp.where(lower_half, partner_coin == 1, partner_coin == 0)
    live_count = jnp.where(crowded, 3 * KEY_LOW, KEY_LOW).astype(jnp.int32)
    orders = jax.vmap(lambda subkey: jax.random.permutation(subkey, FRAMES_DEV))(jax.random.split(key_perm, N_FRAME)).astype(jnp.int32)
    slot_ids = jnp.arange(KEY_SLOTS, dtype=jnp.int32)
    is_live = slot_ids[None, :] < live_count[:, None]
    key_frames = jnp.where(is_live, devices[:, None] * FRAMES_DEV + orders[:, :KEY_SLOTS], -1).reshape(-1)
    ranks_row = jnp.broadcast_to(jnp.arange(FRAMES_DEV, dtype=jnp.int32)[None, :], (N_FRAME, FRAMES_DEV))
    frame_rank = jnp.zeros((N_FRAME, FRAMES_DEV), jnp.int32).at[jnp.broadcast_to(devices[:, None], (N_FRAME, FRAMES_DEV)), orders].set(ranks_row)
    is_key = frame_rank < live_count[:, None]
    offset_side = jax.random.randint(key_side, (N_FRAME, FRAMES_DEV), -1, 2)
    offset_side = jnp.where(frame_rank == KEY_SLOTS, -1, offset_side)
    offset_side = jnp.where(frame_rank == KEY_SLOTS + 1, 1, offset_side)
    target = jnp.clip(devices[:, None] + offset_side, 0, N_FRAME - 1)
    slot_pick = jax.random.randint(key_pick, (N_FRAME, FRAMES_DEV), 0, 3 * KEY_LOW) % live_count[target]
    propagate = jnp.where(is_key, devices[:, None] * KEY_SLOTS + frame_rank, target * KEY_SLOTS + slot_pick).reshape(-1)
    return (key_frames.astype(jnp.int32), propagate.astype(jnp.int32))


def draw_key_frames(key, part):
    return plan_keys(key)[0]


def draw_propagate(key, part):
    return plan_keys(key)[1]


def draw_latents(key, part):
    full_shape = (FRAMES, HEIGHT, WIDTH, C)
    drawn = jax.random.normal(jax.random.fold_in(key, 33), full_shape, jnp.float32)
    return jnp.clip(drawn, -8.0, 8.0).astype(jnp.bfloat16)


def query_key_pair(key):
    first_weights = jax.random.normal(jax.random.fold_in(key, 43), (C, C), jnp.float32) / math.sqrt(C)
    second_weights = jax.random.normal(jax.random.fold_in(key, 44), (C, C), jnp.float32) / math.sqrt(C)
    return (jnp.clip(first_weights, -3.0, 3.0), jnp.clip(second_weights, -3.0, 3.0))


def draw_query_weight(key, part):
    return query_key_pair(key)[0].astype(jnp.bfloat16)


def draw_key_weight(key, part):
    return query_key_pair(key)[1].astype(jnp.bfloat16)


def level_of(stream_key, dims, shards, low, high):
    level = 1.0
    for position, blocks in shards:
        steps = jax.random.uniform(jax.random.fold_in(jax.random.fold_in(stream_key, 6), position), (blocks,), jnp.float32, low / len(shards), high / len(shards))
        level = level * jnp.repeat(jnp.exp(steps), dims[position] // blocks).reshape((-1,) + (1,) * (len(dims) - 1 - position))
    return level


def normal_values(own_key, shape, spread, bound, pieces=(), kind=jnp.bfloat16):
    level = level_of(own_key, shape, pieces, -0.22, 0.18) if pieces else 1.0
    array = jax.random.normal(own_key, shape, jnp.float32) * spread * level
    return jnp.minimum(jnp.maximum(array, -bound), bound).astype(kind)


def setup_inputs(seed: int = 0, part: int = 0) -> dict:
    streams_of = jax.random.split(jax.random.key(seed), 14)
    part_keys = jax.random.split(jax.random.fold_in(streams_of[13], part), 14)
    latents = draw_latents(jax.random.fold_in(jax.random.fold_in(streams_of[13], part), 71), part)
    condition = normal_values(part_keys[1], (KEYS, HEIGHT, WIDTH, C), 1.0, 6.0, ((0, 4), (1, 4)))
    key_frames = draw_key_frames(jax.random.fold_in(jax.random.fold_in(streams_of[13], part), 71), part)
    propagate = draw_propagate(jax.random.fold_in(jax.random.fold_in(streams_of[13], part), 71), part)
    encoder_conv = normal_values(streams_of[4], (9, C, C), (9 * C) ** -0.5, 0.109375)
    zero_conv = normal_values(streams_of[5], (C, C), C ** -0.5, 0.3125)
    attention_gain = jnp.clip(1.0 + 0.15 * jax.random.normal(streams_of[6], (C,), jnp.float32), 0.25, 1.75)
    query_weight = draw_query_weight(jax.random.fold_in(streams_of[13], 71), part)
    key_weight = draw_key_weight(jax.random.fold_in(streams_of[13], 71), part)
    value_weight = normal_values(streams_of[9], (C, C), C ** -0.5, 0.3125)
    output_weight = normal_values(streams_of[10], (C, C), C ** -0.5, 0.3125)
    conv_gain = jnp.clip(1.0 + 0.15 * jax.random.normal(streams_of[11], (C,), jnp.float32), 0.25, 1.75)
    block_conv = normal_values(streams_of[12], (9, C, C), (9 * C) ** -0.5, 0.109375)
    return {"latents": latents, "condition": condition, "key_frames": key_frames, "propagate": propagate, "encoder_conv": encoder_conv, "zero_conv": zero_conv, "attention_gain": attention_gain, "query_weight": query_weight, "key_weight": key_weight, "value_weight": value_weight, "output_weight": output_weight, "conv_gain": conv_gain, "block_conv": block_conv}


def convolve(images, weights):
    frame_count, row_count, col_count, channels = images.shape
    padded = jnp.pad(images, ((0, 0), (1, 1), (1, 1), (0, 0)))
    running = jnp.zeros((frame_count * row_count * col_count, weights.shape[2]), jnp.float32)
    for row_off in range(3):
        for col_off in range(3):
            window = padded[:, row_off:row_off + row_count, col_off:col_off + col_count, :].reshape(-1, channels)
            running = running + jnp.dot(window, weights[3 * row_off + col_off], preferred_element_type=jnp.float32)
    return running.reshape(frame_count, row_count, col_count, -1)

def layer_norm(values_in, scale_gain):
    average = lax.optimization_barrier(jnp.mean(values_in, axis=-1, keepdims=True))
    centered = values_in - average
    variance = lax.optimization_barrier(jnp.mean(centered * centered, axis=-1, keepdims=True))
    return centered * lax.rsqrt(variance + 1e-05) * scale_gain

def positions(frame_total, channels):
    frame_pos = jnp.arange(frame_total, dtype=jnp.float32)[:, None]
    half_index = jnp.arange(channels // 2, dtype=jnp.float32)
    frequency = jnp.exp(half_index * (-2.0 * math.log(10000.0) / channels))
    angles = frame_pos * frequency
    return jnp.stack([jnp.sin(angles), jnp.cos(angles)], axis=-1).reshape(frame_total, channels)

def reference(latents, condition, key_frames, propagate, encoder_conv, zero_conv, attention_gain, query_weight, key_weight, value_weight, output_weight, conv_gain, block_conv):
    encoded = lax.map(lambda single: jax.nn.silu(convolve(single[None], encoder_conv)[0]).astype(jnp.bfloat16), condition)
    keyres = jnp.dot(encoded.reshape(-1, C), zero_conv, preferred_element_type=jnp.float32).astype(jnp.bfloat16).reshape(encoded.shape)
    frame_ids = jnp.arange(FRAMES, dtype=jnp.int32)
    source_frame = key_frames[propagate]
    reach = jnp.exp(-jnp.abs(frame_ids - source_frame).astype(jnp.float32) / (2 * FRAMES_DEV))
    hidden = (latents.astype(jnp.float32) + reach[:, None, None, None] * keyres[propagate].astype(jnp.float32)).astype(jnp.bfloat16)
    encoding = positions(FRAMES, C)

    def attend_row(row_data):
        normed = (layer_norm(row_data.astype(jnp.float32), attention_gain) + encoding[:, None, :]).astype(jnp.bfloat16)
        flattened = normed.reshape(-1, C)
        head_shape = (FRAMES, WIDTH, HEADS, C // HEADS)
        query = jnp.dot(flattened, query_weight, preferred_element_type=jnp.float32).astype(jnp.bfloat16).reshape(head_shape)
        key_proj = jnp.dot(flattened, key_weight, preferred_element_type=jnp.float32).astype(jnp.bfloat16).reshape(head_shape)
        value_proj = jnp.dot(flattened, value_weight, preferred_element_type=jnp.float32).astype(jnp.bfloat16).reshape(head_shape)
        scores = jnp.einsum('fwhd,gwhd->whfg', query.astype(jnp.float32), key_proj.astype(jnp.float32)) / math.sqrt(C // HEADS)
        weights_soft = jax.nn.softmax(scores, axis=-1).astype(jnp.bfloat16)
        mixed_heads = jnp.einsum('whfg,gwhd->fwhd', weights_soft.astype(jnp.float32), value_proj.astype(jnp.float32)).astype(jnp.bfloat16).reshape(-1, C)
        projected = jnp.dot(mixed_heads, output_weight, preferred_element_type=jnp.float32)
        return (row_data.astype(jnp.float32).reshape(-1, C) + projected).astype(jnp.bfloat16).reshape(FRAMES, WIDTH, C)
    attended = jnp.moveaxis(lax.map(attend_row, jnp.moveaxis(hidden, 1, 0)), 0, 1)
    activated = jax.nn.silu(layer_norm(attended.astype(jnp.float32), conv_gain)).astype(jnp.bfloat16)

    def finish(pair_in):
        single_act, single_att = pair_in
        convolved = convolve(single_act[None], block_conv)[0]
        return (single_att.astype(jnp.float32) + convolved).astype(jnp.bfloat16)
    return lax.map(finish, (activated, attended))
```

```python
import functools
import math

import jax
import jax.numpy as jnp
from jax import lax
from jax.experimental import pallas as pl
from jax.experimental.pallas import tpu as pltpu
from jax.sharding import PartitionSpec as P

HEADS = 8
EPS = 1e-05
BF = jnp.bfloat16
F32 = jnp.float32
LOW = -1e30
LANES = 128
MIB = 1 << 20


def kernel_call(body, outs, cost, limit, scratch=(), smem=0, vmem=0, hbm=0, name=None):
    spaces = [pltpu.SMEM] * smem + [pltpu.VMEM] * vmem + [pl.ANY] * hbm
    return pl.pallas_call(
        body,
        out_shape=outs,
        in_specs=[pl.BlockSpec(memory_space=s) for s in spaces],
        out_specs=jax.tree.map(lambda _: pl.BlockSpec(memory_space=pltpu.VMEM), outs),
        scratch_shapes=list(scratch),
        compiler_params=pltpu.CompilerParams(vmem_limit_bytes=limit * MIB),
        cost_estimate=pl.CostEstimate(flops=cost[0], bytes_accessed=cost[1], transcendentals=0),
        name=name,
    )


def dot(a, b):
    return jnp.dot(a, b, preferred_element_type=F32)


def normalized(x, gain):
    centered = x - jnp.mean(x, axis=-1, keepdims=True)
    variance = jnp.mean(centered * centered, axis=-1, keepdims=True)
    return centered * lax.rsqrt(variance + EPS) * gain


def silu(x):
    return x * jax.nn.sigmoid(x)


def lane_pad(x):
    extra = -x.shape[-1] % LANES
    if not extra:
        return x
    return jnp.concatenate([x, jnp.zeros(x.shape[:-1] + (extra,), x.dtype)], axis=-1)


def conv_rows(rows, w_ref, cols):
    count, channels = rows[1].shape
    taps = jnp.concatenate(
        [
            jnp.concatenate([lane_pad(w_ref[3 * r + c]) for c in range(3)], axis=-1)
            for r in range(3)
        ],
        axis=0,
    )
    wide = taps.shape[1] // 3
    full = dot(jnp.concatenate(rows, axis=-1), taps)
    left, mid, right = [full[:, c * wide : c * wide + channels] for c in range(3)]
    col = lax.broadcasted_iota(jnp.int32, (count, 1), 0) % cols
    left = jnp.where(col == 0, 0.0, pltpu.roll(left, 1, 0))
    right = jnp.where(col == cols - 1, 0.0, pltpu.roll(right, count - 1, 0))
    return left + mid + right


def partner(me, k, size):
    return me ^ k if size & (size - 1) == 0 else lax.rem(me + k, size)


def source(me, k, size):
    return me ^ k if size & (size - 1) == 0 else lax.rem(me + size - k, size)


def swap(x, axis, k):
    size = lax.axis_size(axis)
    if size & (size - 1) == 0:
        pairs = [(i, i ^ k) for i in range(size)]
    else:
        pairs = [(i, (i + k) % size) for i in range(size)]
    return lax.ppermute(x, axis, pairs)


def pairing(x, axis, odd):
    size = lax.axis_size(axis)
    pairs = []
    for i in range(1 if odd else 0, size - 1, 2):
        pairs += [(i, i + 1), (i + 1, i)]
    if not pairs:
        return jnp.zeros_like(x)
    return lax.ppermute(x, axis, pairs)


def parity_of():
    return lax.rem(lax.axis_index("row"), 2)


def window(me, k, n, width):
    if n == 1:
        return pl.ds(0, width)
    return pl.ds(pl.multiple_of(me * width, width), width)


def cut_body(n, cond_ref, lat_ref, ea_ref, eb_ref, *refs):
    outs, sems = refs[:n], refs[n]
    me, parity = lax.axis_index("frame"), parity_of()
    last = cond_ref.shape[1] - 1
    width = lat_ref.shape[2] // n
    copies = [
        pltpu.make_async_copy(cond_ref.at[:, last * (1 - parity)], ea_ref, sems.at[0]),
        pltpu.make_async_copy(cond_ref.at[:, last * parity], eb_ref, sems.at[1]),
    ]
    for k in range(n):
        cut = window(partner(me, k, n), k, n, width)
        copies.append(pltpu.make_async_copy(lat_ref.at[:, :, cut, :], outs[k], sems.at[2 + k]))
    for copy in copies:
        copy.start()
    for copy in copies:
        copy.wait()


def encoder_body(n, cond_ref, ha_ref, hb_ref, w_ref, zero_ref, *refs):
    outs, res, edge = refs[:n], refs[n], refs[n + 1]
    slots, nrows, cols, channels = cond_ref.shape
    parity = parity_of()
    edge[1 - parity] = ha_ref[...]
    edge[parity] = hb_ref[...]
    rows = [edge[0]] + [cond_ref[:, r] for r in range(nrows)] + [edge[1]]
    rows = [r.reshape(slots * cols, channels) for r in rows]
    for r in range(nrows):
        feat = silu(conv_rows(rows[r : r + 3], w_ref, cols)).astype(BF)
        res[:, r] = dot(feat, zero_ref[...]).astype(BF).reshape(slots, cols, channels)
    for k in range(n):
        me = partner(lax.axis_index("frame"), k, n) if n > 1 else 0
        outs[k][...] = res[:, :, window(me, k, n, cols // n), :]


def gathered(ref, rows):
    return jnp.concatenate([ref[t, rows, :] for t in range(ref.shape[0])], axis=-1)


def attention_body(n, kf_ref, prop_ref, *refs):
    lat = refs[:n]
    res = refs[n : 2 * n]
    gain_ref, wq_ref, wk_ref, wv_ref, wo_ref = refs[2 * n : 2 * n + 5]
    outs = refs[2 * n + 5 : 3 * n + 5]
    keyres, hid, tok, qs, ks, vs, ms = refs[3 * n + 5 :]
    frames_dev, pix, channels = lat[0].shape
    slots = res[0].shape[0]
    frames = frames_dev * n
    head_dim = channels // HEADS
    me = lax.axis_index("frame")
    for k in range(n):
        first = source(me, k, n) * slots
        for j in range(slots):
            keyres[first + j] = res[k][j]
    half = lax.broadcasted_iota(jnp.int32, (1, channels), 1)
    freq = jnp.exp((half // 2).astype(F32) * (-2.0 * math.log(10000.0) / channels))
    for k in range(n):
        base = source(me, k, n) * frames_dev
        rows = lax.broadcasted_iota(jnp.int32, (frames_dev, channels), 0) + base
        angle = rows.astype(F32) * freq
        code = jnp.where(half % 2 == 0, jnp.sin(angle), jnp.cos(angle))
        for j in range(frames_dev):
            frame = base + j
            slot = prop_ref[frame]
            gap = jnp.abs(frame - kf_ref[slot]).astype(F32)
            reach = jnp.exp(jnp.full((1, channels), -gap / (2 * frames_dev), F32))
            value = lat[k][j].astype(F32) + reach * keyres[slot].astype(F32)
            hidden = value.astype(BF).astype(F32)
            at = k * frames_dev + j
            hid[at] = hidden
            normed = lane_pad(normalized(hidden, gain_ref[...][None]) + code[j : j + 1])
            for t in range(tok.shape[0]):
                tok[t, pl.ds(at * pix, pix), :] = normed[:, t * LANES : (t + 1) * LANES]
    for p in range(0, pix, 2):
        pair = [gathered(tok, pl.ds(p + i, frames, stride=pix)) for i in range(2)]
        x = jnp.concatenate(pair, axis=0)[:, :channels].astype(BF)
        qs[pl.ds(p * frames, 2 * frames), :] = x
    x = qs[...]
    ks[...] = dot(x, wk_ref[...]).astype(BF)
    vs[...] = dot(x, wv_ref[...]).astype(BF)
    qs[...] = dot(x, wq_ref[...]).astype(BF)
    group = max(d for d in range(1, pix + 1) if pix % d == 0 and (d == 1 or d * frames <= LANES))
    tokens = frames * group
    lane = lax.broadcasted_iota(jnp.int32, (1, channels), 1)
    same = (lax.broadcasted_iota(jnp.int32, (tokens, tokens), 0) // frames) == (
        lax.broadcasted_iota(jnp.int32, (tokens, tokens), 1) // frames
    )
    scale = math.log2(math.e) / math.sqrt(head_dim)
    for g in range(pix // group):
        at = pl.ds(g * tokens, tokens)
        q, kk, v = qs[at, :], ks[at, :], vs[at, :]
        tiles = [None] * (-(-channels // LANES))
        for h in range(HEADS):
            low, high = h * head_dim, (h + 1) * head_dim
            a = low // LANES * LANES
            b = min(-(-high // LANES) * LANES, channels)
            inside = (lane[:, a:b] >= low) & (lane[:, a:b] < high)
            kh = jnp.where(inside, kk[:, a:b], 0)
            vh = jnp.where(inside, v[:, a:b], 0)
            s = lax.dot_general(q[:, a:b], kh, (((1,), (1,)), ((), ())), preferred_element_type=F32)
            if group > 1:
                s = jnp.where(same, s, LOW)
            p = jnp.exp2((s - jnp.max(s, axis=-1, keepdims=True)) * scale)
            p = (p * (1.0 / jnp.sum(p, axis=-1, keepdims=True))).astype(BF)
            o = dot(p, vh)
            for t in range(a // LANES, -(-b // LANES)):
                piece = o[:, t * LANES - a : min((t + 1) * LANES, b) - a]
                tiles[t] = piece if tiles[t] is None else tiles[t] + piece
        ms[at, :] = jnp.concatenate(tiles, axis=-1).astype(BF)
    projected = lane_pad(dot(ms[...], wo_ref[...]))
    for t in range(tok.shape[0]):
        tok[t] = projected[:, t * LANES : (t + 1) * LANES]
    for k in range(n):
        for j in range(frames_dev):
            at = k * frames_dev + j
            mixed = gathered(tok, pl.ds(at, pix, stride=frames))[:, :channels]
            outs[k][j] = (hid[at] + mixed).astype(BF)


def activation_body(n, *refs):
    pieces = refs[:n]
    gain_ref, att_ref, act_ref, ea_ref, eb_ref = refs[n:]
    frames_dev, nrows, width, channels = pieces[0].shape
    parity = parity_of()
    for k in range(n):
        me = source(lax.axis_index("frame"), k, n) if n > 1 else 0
        at = window(me, k, n, width)
        piece = pieces[k][...]
        att_ref[:, :, at, :] = piece
        act = silu(normalized(piece.astype(F32), gain_ref[...].reshape(1, 1, 1, channels)))
        act_ref[:, :, at, :] = act.astype(BF)
    ea_ref[...] = act_ref[:, (nrows - 1) * (1 - parity)]
    eb_ref[...] = act_ref[:, (nrows - 1) * parity]


def block_body(att_ref, act_ref, ha_ref, hb_ref, w_ref, out_ref, edge):
    frames_dev, nrows, cols, channels = act_ref.shape
    parity = parity_of()
    edge[1 - parity] = ha_ref[...]
    edge[parity] = hb_ref[...]
    rows = [edge[0]] + [act_ref[:, r] for r in range(nrows)] + [edge[1]]
    rows = [r.reshape(frames_dev * cols, channels) for r in rows]
    for r in range(nrows):
        conv = conv_rows(rows[r : r + 3], w_ref, cols).reshape(frames_dev, cols, channels)
        out_ref[:, r] = (att_ref[:, r].astype(F32) + conv).astype(BF)


def shards(
    latents,
    condition,
    key_frames,
    propagate,
    encoder_conv,
    zero_conv,
    attention_gain,
    query_weight,
    key_weight,
    value_weight,
    output_weight,
    conv_gain,
    block_conv,
):
    frames_dev, nrows, cols, channels = latents.shape
    slots = condition.shape[0]
    n = lax.axis_size("frame")
    width = cols // n
    frames, pix = frames_dev * n, nrows * width
    me, parity = lax.axis_index("frame"), parity_of()
    sds = jax.ShapeDtypeStruct
    aligned = width % 16 == 0
    parts = n if aligned else 1
    order = [source(me, k, n) for k in range(n)]

    def cut(x, k):
        start = partner(me, k, n) * width
        return lax.dynamic_slice_in_dim(x, start, width, axis=2)

    def flat(x):
        return x.reshape(x.shape[0], pix, channels)

    if aligned:
        edge = sds((slots, cols, channels), BF)
        cond_a, cond_b, *lat = kernel_call(
            functools.partial(cut_body, n),
            [edge, edge] + [sds((frames_dev, nrows, width, channels), BF)] * n,
            (0, 2 * MIB),
            6,
            [pltpu.SemaphoreType.DMA((n + 2,))],
            hbm=2,
            name="cut",
        )(condition, latents)
    else:
        last = nrows - 1
        cond_a = lax.dynamic_index_in_dim(condition, last * (1 - parity), 1, keepdims=False)
        cond_b = lax.dynamic_index_in_dim(condition, last * parity, 1, keepdims=False)
        lat = [cut(latents, k) for k in range(n)]
    halo_a = pairing(cond_a, "row", False)
    halo_b = pairing(cond_b, "row", True)
    lat = [lat[0]] + [swap(lat[k], "frame", k) for k in range(1, n)]
    res = kernel_call(
        functools.partial(encoder_body, parts),
        [sds((slots, nrows, cols // parts, channels), BF)] * parts,
        (2 * slots * nrows * cols * channels * channels * 10, 4 * MIB),
        20,
        [
            pltpu.VMEM((slots, nrows, cols, channels), BF),
            pltpu.VMEM((2, slots, cols, channels), BF),
        ],
        vmem=5,
        name="encoder",
    )(condition, halo_a, halo_b, encoder_conv, zero_conv)
    if not aligned:
        res = [cut(res[0], k) for k in range(n)]
    res = [res[0]] + [swap(res[k], "frame", k) for k in range(1, n)]
    tokens = pltpu.VMEM((frames * pix, channels), BF)
    att = kernel_call(
        functools.partial(attention_body, n),
        [sds((frames_dev, pix, channels), BF)] * n,
        (2 * frames * pix * channels * channels * 8, 4 * MIB),
        24,
        [
            pltpu.VMEM((slots * n, pix, channels), BF),
            pltpu.VMEM((frames, pix, channels), F32),
            pltpu.VMEM((-(-channels // LANES), frames * pix, LANES), F32),
            tokens,
            tokens,
            tokens,
            tokens,
        ],
        smem=2,
        vmem=2 * n + 5,
        name="attention",
    )(
        key_frames,
        propagate,
        *map(flat, lat),
        *map(flat, res),
        attention_gain,
        query_weight,
        key_weight,
        value_weight,
        output_weight,
    )
    att = [a.reshape(frames_dev, nrows, width, channels) for a in att]
    att = [att[0]] + [swap(att[k], "frame", k) for k in range(1, n)]
    if not aligned:
        att = jnp.stack(att)[jnp.stack(order)]
        att = [jnp.moveaxis(att, 0, 2).reshape(latents.shape)]
    whole = sds(latents.shape, BF)
    edge = sds((frames_dev, cols, channels), BF)
    attended, activated, edge_a, edge_b = kernel_call(
        functools.partial(activation_body, parts),
        [whole, whole, edge, edge],
        (10 * frames_dev * nrows * cols * channels, 2 * MIB),
        12,
        vmem=parts + 1,
        name="activation",
    )(*att, conv_gain)
    halo_a = pairing(edge_a, "row", False)
    halo_b = pairing(edge_b, "row", True)
    return kernel_call(
        block_body,
        whole,
        (2 * frames_dev * nrows * cols * channels * channels * 9, 4 * MIB),
        24,
        [pltpu.VMEM((2, frames_dev, cols, channels), BF)],
        vmem=5,
        name="block",
    )(attended, activated, halo_a, halo_b, block_conv)


def solution(mesh):
    image = P(("group", "frame"), "row", None, None)
    placed = (image, image, P("group"), P("group")) + (P(),) * 9
    return jax.shard_map(shards, mesh=mesh, in_specs=placed, out_specs=image, check_vma=False)
```

```python
import functools
import math

import jax
import jax.numpy as jnp
from jax import lax
from jax.experimental import pallas as pl
from jax.experimental.pallas import tpu as pltpu
from jax.sharding import PartitionSpec as P

HEADS = 8
EPS = 1e-05
BF = jnp.bfloat16
F32 = jnp.float32
LOW = -1e30
LANES = 128
MIB = 1 << 20


def kernel_call(body, outs, cost, limit, scratch=(), smem=0, vmem=0, hbm=0, name=None):
    spaces = [pltpu.SMEM] * smem + [pltpu.VMEM] * vmem + [pltpu.HBM] * hbm
    return pl.pallas_call(
        body,
        out_shape=outs,
        in_specs=[pl.BlockSpec(memory_space=s) for s in spaces],
        out_specs=jax.tree.map(lambda _: pl.BlockSpec(memory_space=pltpu.VMEM), outs),
        scratch_shapes=list(scratch),
        compiler_params=pltpu.CompilerParams(vmem_limit_bytes=limit * MIB),
        cost_estimate=pl.CostEstimate(flops=cost[0], bytes_accessed=cost[1], transcendentals=0),
        name=name,
    )


def dot(a, b):
    return jnp.dot(a, b, preferred_element_type=F32)


def normalized(x, gain):
    centered = x - jnp.mean(x, axis=-1, keepdims=True)
    variance = jnp.mean(centered * centered, axis=-1, keepdims=True)
    return centered * lax.rsqrt(variance + EPS) * gain


def silu(x):
    return x * jax.nn.sigmoid(x)


def lane_pad(x):
    extra = -x.shape[-1] % LANES
    if not extra:
        return x
    return jnp.concatenate([x, jnp.zeros(x.shape[:-1] + (extra,), x.dtype)], axis=-1)


def taps_of(w_ref, row):
    return jnp.concatenate([lane_pad(w_ref[3 * row + c]) for c in range(3)], axis=-1)


def col_shifts(full, channels, cols):
    count, wide = full.shape[0], full.shape[1] // 3
    left, mid, right = [full[:, c * wide : c * wide + channels] for c in range(3)]
    col = lax.broadcasted_iota(jnp.int32, (count, 1), 0) % cols
    left = jnp.where(col == 0, 0.0, pltpu.roll(left, 1, 0))
    right = jnp.where(col == cols - 1, 0.0, pltpu.roll(right, count - 1, 0))
    return left + mid + right


def conv_own(rows, w_ref, r, cols):
    near = [i for i in (r - 1, r, r + 1) if 0 <= i < len(rows)]
    taps = jnp.concatenate([taps_of(w_ref, i - r + 1) for i in near], axis=0)
    full = dot(jnp.concatenate([rows[i] for i in near], axis=-1), taps)
    return col_shifts(full, rows[0].shape[1], cols)


def conv_edge(halo, w_ref, row, cols):
    return col_shifts(dot(halo, taps_of(w_ref, row)), halo.shape[1], cols)


def positions(frames, channels):
    frame = jnp.arange(frames, dtype=F32)[:, None]
    freq = jnp.exp(jnp.arange(channels // 2, dtype=F32) * (-2.0 * math.log(10000.0) / channels))
    angles = frame * freq
    return jnp.stack([jnp.sin(angles), jnp.cos(angles)], axis=-1).reshape(frames, channels)


def partner(me, k, size):
    return me ^ k if size & (size - 1) == 0 else lax.rem(me + k, size)


def source(me, k, size):
    return me ^ k if size & (size - 1) == 0 else lax.rem(me + size - k, size)


def swap(x, axis, k):
    size = lax.axis_size(axis)
    if size & (size - 1) == 0:
        pairs = [(i, i ^ k) for i in range(size)]
    else:
        pairs = [(i, (i + k) % size) for i in range(size)]
    return lax.ppermute(x, axis, pairs)


def pairing(x, axis, odd):
    size = lax.axis_size(axis)
    pairs = []
    for i in range(1 if odd else 0, size - 1, 2):
        pairs += [(i, i + 1), (i + 1, i)]
    if not pairs:
        return jnp.zeros_like(x)
    return lax.ppermute(x, axis, pairs)


def parity_of():
    return lax.rem(lax.axis_index("row"), 2)


def sided(near, far):
    even = parity_of() == 0
    return jnp.where(even, far, near), jnp.where(even, near, far)


def window(me, k, n, width):
    if n == 1:
        return pl.ds(0, width)
    return pl.ds(pl.multiple_of(me * width, width), width)


def cut_body(n, cond_ref, lat_ref, ea_ref, eb_ref, *refs):
    outs, sems = refs[:n], refs[n]
    me, parity = lax.axis_index("frame"), parity_of()
    last = cond_ref.shape[1] - 1
    width = lat_ref.shape[2] // n
    copies = [
        pltpu.make_async_copy(cond_ref.at[:, last * (1 - parity)], ea_ref, sems.at[0]),
        pltpu.make_async_copy(cond_ref.at[:, last * parity], eb_ref, sems.at[1]),
    ]
    for k in range(n):
        cut = window(partner(me, k, n), k, n, width)
        copies.append(pltpu.make_async_copy(lat_ref.at[:, :, cut, :], outs[k], sems.at[2 + k]))
    for copy in copies:
        copy.start()
    for copy in copies:
        copy.wait()


def encoder_own_body(cond_hbm, w_hbm, zero_hbm, acc_ref, w_ref, zero_ref, cond_ref, sems):
    copies = [
        pltpu.make_async_copy(cond_hbm, cond_ref, sems.at[0]),
        pltpu.make_async_copy(w_hbm, w_ref, sems.at[1]),
        pltpu.make_async_copy(zero_hbm, zero_ref, sems.at[2]),
    ]
    for copy in copies:
        copy.start()
    for copy in copies:
        copy.wait()
    slots, nrows, cols, channels = cond_ref.shape
    rows = [cond_ref[:, r].reshape(slots * cols, channels) for r in range(nrows)]
    for r in range(nrows):
        acc_ref[r] = conv_own(rows, w_ref, r, cols)


def encoder_edge_body(n, acc_ref, ha_ref, hb_ref, w_ref, zero_ref, *refs):
    outs, res = refs[:n], refs[n]
    slots, nrows, cols, channels = res.shape
    edge = sided(ha_ref[...], hb_ref[...])
    for r in range(nrows):
        total = acc_ref[r]
        if r == 0:
            total = total + conv_edge(edge[0].reshape(-1, channels), w_ref, 0, cols)
        if r == nrows - 1:
            total = total + conv_edge(edge[1].reshape(-1, channels), w_ref, 2, cols)
        feat = silu(total).astype(BF)
        res[:, r] = dot(feat, zero_ref[...]).astype(BF).reshape(slots, cols, channels)
    for k in range(n):
        me = partner(lax.axis_index("frame"), k, n) if n > 1 else 0
        outs[k][...] = res[:, :, window(me, k, n, cols // n), :]


def gathered(ref, rows):
    return jnp.concatenate([ref[t, rows, :] for t in range(ref.shape[0])], axis=-1)


def attention_body(n, kf_ref, prop_ref, *refs):
    lat = refs[:n]
    res = refs[n : 2 * n]
    code_ref, gain_ref, wq_ref, wk_ref, wv_ref, wo_ref = refs[2 * n : 2 * n + 6]
    outs = refs[2 * n + 6 : -9]
    keyres, hid, tok, qs, ks, vs, bias, scores, probs = refs[-9:]
    frames_dev, pix, channels = lat[0].shape
    slots = res[0].shape[0]
    frames = frames_dev * n
    head_dim = channels // HEADS
    me = lax.axis_index("frame")
    for k in range(n):
        first = source(me, k, n) * slots
        for j in range(slots):
            keyres[first + j] = res[k][j]
    for k in range(n):
        home = source(me, k, n)
        code = code_ref[home]
        for j in range(frames_dev):
            frame = home * frames_dev + j
            slot = prop_ref[frame]
            gap = jnp.abs(frame - kf_ref[slot]).astype(F32)
            reach = jnp.exp(jnp.full((1, channels), -gap / (2 * frames_dev), F32))
            value = lat[k][j].astype(F32) + reach * keyres[slot].astype(F32)
            hidden = value.astype(BF).astype(F32)
            at = k * frames_dev + j
            hid[at] = hidden
            normed = lane_pad(normalized(hidden, gain_ref[...][None]) + code[j : j + 1])
            for t in range(tok.shape[0]):
                tok[t, pl.ds(at * pix, pix), :] = normed[:, t * LANES : (t + 1) * LANES]
    for p in range(0, pix, 2):
        pair = [gathered(tok, pl.ds(p + i, frames, stride=pix)) for i in range(2)]
        x = jnp.concatenate(pair, axis=0)[:, :channels].astype(BF)
        qs[pl.ds(p * frames, 2 * frames), :] = x
    weights = [lane_pad(w[...]) for w in (wq_ref, wk_ref, wv_ref)]
    qkv = dot(qs[...], jnp.concatenate(weights, axis=-1))
    wide = qkv.shape[1] // 3
    for i, ref in enumerate((qs, ks, vs)):
        ref[...] = qkv[:, i * wide : i * wide + channels].astype(BF)
    group = max(d for d in range(1, pix + 1) if pix % d == 0 and (d == 1 or d * frames <= LANES))
    tokens = frames * group
    wide = bias.shape[1]
    lane = lax.broadcasted_iota(jnp.int32, (1, channels), 1)
    row_pix = lax.broadcasted_iota(jnp.int32, (tokens, wide), 0) // frames
    col_pix = lax.broadcasted_iota(jnp.int32, (tokens, wide), 1) // frames
    bias[...] = jnp.where(row_pix == col_pix, 0.0, LOW)
    scale = math.log2(math.e) / math.sqrt(head_dim)

    def span(pair):
        low, high = pair * head_dim, (pair + 2) * head_dim
        return low // LANES * LANES, min(-(-high // LANES) * LANES, channels)

    def stacked(x, pair):
        a, b = span(pair)
        fill = jnp.zeros((wide - tokens, b - a), x.dtype)
        rows = []
        for h in (pair, pair + 1):
            inside = (lane[:, a:b] >= h * head_dim) & (lane[:, a:b] < (h + 1) * head_dim)
            rows += [jnp.where(inside, x[:, a:b], 0)] + ([fill] if wide > tokens else [])
        return jnp.concatenate(rows, axis=0)

    def score(g):
        at = pl.ds(g * tokens, tokens)
        q, kk = qs[at, :], ks[at, :]
        for pair in range(0, HEADS, 2):
            a, b = span(pair)
            s = lax.dot_general(
                q[:, a:b],
                stacked(kk, pair),
                (((1,), (1,)), ((), ())),
                preferred_element_type=F32,
            )
            scores[g % 2, :, pair * wide : (pair + 2) * wide] = s

    def weigh(g):
        for h in range(HEADS):
            s = scores[g % 2, :, h * wide : (h + 1) * wide] + bias[...]
            p = jnp.exp2((s - jnp.max(s, axis=-1, keepdims=True)) * scale)
            p = p * (1.0 / jnp.sum(p, axis=-1, keepdims=True))
            probs[g % 2, :, h * wide : (h + 1) * wide] = p.astype(BF)

    def mix(g):
        at = pl.ds(g * tokens, tokens)
        v = vs[at, :]
        tiles = [None] * (-(-channels // LANES))
        for pair in range(0, HEADS, 2):
            a, b = span(pair)
            o = dot(probs[g % 2, :, pair * wide : (pair + 2) * wide], stacked(v, pair))
            for t in range(a // LANES, -(-b // LANES)):
                piece = o[:, t * LANES - a : min((t + 1) * LANES, b) - a]
                tiles[t] = piece if tiles[t] is None else tiles[t] + piece
        vs[at, :] = jnp.concatenate(tiles, axis=-1).astype(BF)

    groups = pix // group
    for step in range(groups + 2):
        if step < groups:
            score(step)
        if 0 <= step - 1 < groups:
            weigh(step - 1)
        if 0 <= step - 2:
            mix(step - 2)
    projected = lane_pad(dot(vs[...], wo_ref[...]))
    for t in range(tok.shape[0]):
        tok[t] = projected[:, t * LANES : (t + 1) * LANES]
    for k in range(n):
        for j in range(frames_dev):
            at = k * frames_dev + j
            mixed = gathered(tok, pl.ds(at, pix, stride=frames))[:, :channels]
            piece = len(outs) // n * j // frames_dev
            row = j - frames_dev * piece // (len(outs) // n)
            outs[piece * n + k][row] = (hid[at] + mixed).astype(BF)


def activation_body(n, *refs):
    pieces = refs[:n]
    gain_ref, att_ref, act_ref, ea_ref, eb_ref = refs[n:]
    frames_dev, nrows, width, channels = pieces[0].shape
    parity = parity_of()
    for k in range(n):
        me = source(lax.axis_index("frame"), k, n) if n > 1 else 0
        at = window(me, k, n, width)
        piece = pieces[k][...]
        att_ref[:, :, at, :] = piece
        act = silu(normalized(piece.astype(F32), gain_ref[...].reshape(1, 1, 1, channels)))
        act_ref[:, :, at, :] = act.astype(BF)
    ea_ref[...] = act_ref[:, (nrows - 1) * (1 - parity)]
    eb_ref[...] = act_ref[:, (nrows - 1) * parity]


def block_own_body(att_ref, act_ref, w_ref, acc_ref):
    count, nrows, cols, channels = act_ref.shape
    rows = [act_ref[:, r].reshape(count * cols, channels) for r in range(nrows)]
    for r in range(nrows):
        conv = conv_own(rows, w_ref, r, cols).reshape(count, cols, channels)
        acc_ref[:, r] = att_ref[:, r].astype(F32) + conv


def block_edge_body(m, *refs):
    accs, near, far = refs[:m], refs[m : 2 * m], refs[2 * m : 3 * m]
    w_ref, out_ref = refs[3 * m :]
    for i in range(m):
        count, nrows, cols, channels = accs[i].shape
        edge = sided(near[i][...], far[i][...])
        for r in range(nrows):
            total = accs[i][:, r]
            for side, at in ((0, 0), (1, nrows - 1)):
                if r == at:
                    conv = conv_edge(edge[side].reshape(-1, channels), w_ref, 2 * side, cols)
                    total = total + conv.reshape(count, cols, channels)
            out_ref[pl.ds(i * count, count), r] = total.astype(BF)


def shards(
    latents,
    condition,
    key_frames,
    propagate,
    encoder_conv,
    zero_conv,
    attention_gain,
    query_weight,
    key_weight,
    value_weight,
    output_weight,
    conv_gain,
    block_conv,
):
    frames_dev, nrows, cols, channels = latents.shape
    slots = condition.shape[0]
    n = lax.axis_size("frame")
    width = cols // n
    frames, pix = frames_dev * n, nrows * width
    me, parity = lax.axis_index("frame"), parity_of()
    sds = jax.ShapeDtypeStruct
    aligned = width % 16 == 0
    parts = n if aligned else 1
    order = [source(me, k, n) for k in range(n)]

    def cut(x, k):
        start = partner(me, k, n) * width
        return lax.dynamic_slice_in_dim(x, start, width, axis=2)

    def flat(x):
        return x.reshape(x.shape[0], pix, channels)

    if aligned:
        edge = sds((slots, cols, channels), BF)
        cond_a, cond_b, *lat = kernel_call(
            functools.partial(cut_body, n),
            [edge, edge] + [sds((frames_dev, nrows, width, channels), BF)] * n,
            (0, 2 * MIB),
            6,
            [pltpu.SemaphoreType.DMA((n + 2,))],
            hbm=2,
            name="cut",
        )(condition, latents)
    else:
        last = nrows - 1
        cond_a = lax.dynamic_index_in_dim(condition, last * (1 - parity), 1, keepdims=False)
        cond_b = lax.dynamic_index_in_dim(condition, last * parity, 1, keepdims=False)
        lat = [cut(latents, k) for k in range(n)]
    halo_a = pairing(cond_a, "row", False)
    halo_b = pairing(cond_b, "row", True)
    lat = [lat[0]] + [swap(lat[k], "frame", k) for k in range(1, n)]
    macs = nrows * cols * channels * channels
    vmem = pltpu.VMEM
    acc, enc_w, zero_w = kernel_call(
        encoder_own_body,
        [
            sds((nrows, slots * cols, channels), F32),
            sds(encoder_conv.shape, BF),
            sds(zero_conv.shape, BF),
        ],
        (12 * slots * macs, 4 * MIB),
        16,
        [vmem(condition.shape, BF), pltpu.SemaphoreType.DMA((3,))],
        hbm=3,
        name="encoder_own",
    )(condition, encoder_conv, zero_conv)
    res = kernel_call(
        functools.partial(encoder_edge_body, parts),
        [sds((slots, nrows, cols // parts, channels), BF)] * parts,
        (8 * slots * macs, 4 * MIB),
        16,
        [vmem(condition.shape, BF)],
        vmem=5,
        name="encoder_edge",
    )(acc, halo_a, halo_b, enc_w, zero_w)
    if not aligned:
        res = [cut(res[0], k) for k in range(n)]
    res = [res[0]] + [swap(res[k], "frame", k) for k in range(1, n)]
    code = positions(frames, channels).reshape(n, frames_dev, channels)
    halves = 2 if frames_dev % 2 == 0 else 1
    share = frames_dev // halves
    tokens = vmem((frames * pix, channels), BF)
    group = max(d for d in range(1, pix + 1) if pix % d == 0 and (d == 1 or d * frames <= LANES))
    wide = -(-group * frames // LANES) * LANES
    pieces = kernel_call(
        functools.partial(attention_body, n),
        [sds((share, pix, channels), BF)] * (halves * n),
        (2 * frames * pix * channels * channels * 8, 4 * MIB),
        24,
        [
            vmem((slots * n, pix, channels), BF),
            vmem((frames, pix, channels), F32),
            vmem((-(-channels // LANES), frames * pix, LANES), F32),
            tokens,
            tokens,
            tokens,
            vmem((group * frames, wide), F32),
            vmem((2, group * frames, HEADS * wide), F32),
            vmem((2, group * frames, HEADS * wide), BF),
        ],
        smem=2,
        vmem=2 * n + 6,
        name="attention",
    )(
        key_frames,
        propagate,
        *map(flat, lat),
        *map(flat, res),
        code,
        attention_gain,
        query_weight,
        key_weight,
        value_weight,
        output_weight,
    )
    shape = (share, nrows, cols, channels)
    accs, near, far = [], [], []
    for i in range(halves):
        att = [p.reshape(share, nrows, width, channels) for p in pieces[i * n : (i + 1) * n]]
        att = [att[0]] + [swap(att[k], "frame", k) for k in range(1, n)]
        if not aligned:
            att = jnp.stack(att)[jnp.stack(order)]
            att = [jnp.moveaxis(att, 0, 2).reshape(shape)]
        edge = sds((share, cols, channels), BF)
        attended, activated, edge_a, edge_b = kernel_call(
            functools.partial(activation_body, parts),
            [sds(shape, BF), sds(shape, BF), edge, edge],
            (10 * share * nrows * cols * channels, 2 * MIB),
            8,
            vmem=parts + 1,
            name="activation",
        )(*att, conv_gain)
        near.append(pairing(edge_a, "row", False))
        far.append(pairing(edge_b, "row", True))
        accs.append(
            kernel_call(
                block_own_body,
                sds(shape, F32),
                (12 * share * macs, 4 * MIB),
                16,
                vmem=3,
                name="block_own",
            )(attended, activated, block_conv)
        )
    return kernel_call(
        functools.partial(block_edge_body, halves),
        sds(latents.shape, BF),
        (6 * frames_dev * macs, 4 * MIB),
        20,
        vmem=3 * halves + 1,
        name="block_edge",
    )(*accs, *near, *far, block_conv)


def solution(mesh):
    image = P(("group", "frame"), "row", None, None)
    placed = (image, image, P("group"), P("group")) + (P(),) * 9
    return jax.shard_map(shards, mesh=mesh, in_specs=placed, out_specs=image, check_vma=False)
```
